256 devices in a mesh: sector: 16 (over x, y_lo, core), block: 16 (over z, y_hi).
Axes of the slice: x: 4, y: 4 (y_hi: 2, y_lo: 2; y = y_hi * 2 + y_lo), z: 8, core: 2. Of those that a mesh axis runs over, the one named last changes fastest.
Arguments:
- flow: float32 [5, 4, 256, 2048], P(None, None, 'block', 'sector'), may hold values from -1 to 5, as said below
- adjoint: float32 [5, 4, 256, 2048], P(None, None, 'block', 'sector'), may hold values from -6 to 6
- adjoint_later: float32 [2, 5, 4, 256, 2048], P(None, None, None, 'block', 'sector'), may hold values from -6 to 6
- objective_grad: float32 [5, 4, 256, 2048], P(None, None, 'block', 'sector'), may hold values from -12 to 12
- volume: float32 [4, 256, 2048], P(None, 'block', 'sector'), may hold values from 0.5 to 2
- panel_maps: float32 [4, 4, 128, 128], replicated, may hold values from 0 to 1, as said below
- rotor_step: int32 [1], replicated, may hold values from 0 to 63
Outputs:
- updated_adjoint: float32 [5, 4, 256, 2048], P(None, None, 'block', 'sector')
The draws below stay inside these ranges and needn't reach their ends.
Inputs may be any that keep to these rules, and one draw needn't show every extreme that they name: `flow`: density and pressure are positive in every cell. `panel_maps`: entries are non-negative.
All inputs are finite; a program needn't handle non-finite values.
Results may differ from the reference program's by a relative error of at most 0.000057.
Values sent between devices are 32-bit elements; how exact they have to be, the bound alone decides.
A program may use at most 64 MiB of HBM per device.

```python
import math
import jax
import jax.numpy as jnp
from jax import lax

LAYERS = 4
CIRC_DEV = 128
PHASES = 4
ITERS = 4
SECTORS = 16
NX = 256
NT = 2048


def draw_flow(key, part):
    keys = jax.random.split(jax.random.fold_in(key, 11), 5)
    shape = (LAYERS, NX, NT)
    density = jax.random.uniform(keys[0], shape, jnp.float32, 0.6, 1.6)
    pressure_field = jax.random.uniform(keys[4], shape, jnp.float32, 0.5, 1.5)
    axial_speed = jax.random.uniform(keys[1], shape, jnp.float32, 0.2, 0.8)
    swirl_speed = jax.random.uniform(keys[2], shape, jnp.float32, -0.5, 0.5)
    radial_speed = jax.random.uniform(keys[3], shape, jnp.float32, -0.2, 0.2)
    energy = pressure_field / 0.4 + 0.5 * density * (axial_speed * axial_speed + swirl_speed * swirl_speed + radial_speed * radial_speed)
    return jnp.stack([density, density * axial_speed, density * swirl_speed, density * radial_speed, energy])


def draw_panel_maps(key, part):
    keys = jax.random.split(jax.random.fold_in(key, 23), 3)
    weight_share = jax.random.uniform(keys[0], (PHASES, 2), jnp.float32, 0.2, 0.8)
    shares = jnp.stack([1.0 - weight_share[:, 0], weight_share[:, 0], 1.0 - weight_share[:, 1], weight_share[:, 1]], axis=1)
    diagonal_part = jax.random.uniform(keys[1], (PHASES, 4, 1, 1), jnp.float32, 0.5, 0.8)
    spread = jax.random.uniform(keys[2], (PHASES, 4, CIRC_DEV, CIRC_DEV), jnp.float32, 0.0, 2.0)
    identity_part = jnp.eye(CIRC_DEV, dtype=jnp.float32)
    return shares[:, :, None, None] * (diagonal_part * identity_part + (1.0 - diagonal_part) * spread / CIRC_DEV)


def block_levels(own_key, dims, pieces, low, top_value):
    factor_of, own = 1.0, jax.random.fold_in(own_key, 6)
    for axis_at, parts in pieces:
        steps = jnp.exp(jax.random.uniform(jax.random.fold_in(own, axis_at), (parts,), jnp.float32, low / len(pieces), top_value / len(pieces)))
        factor_of = factor_of * jnp.repeat(steps, dims[axis_at] // parts).reshape([-1 if axis == axis_at else 1 for axis in range(len(dims))])
    return factor_of


def bell_draw(key, shape, width, reach, cuts=(), held_as=jnp.bfloat16):
    entries = width * jax.random.normal(key, shape, jnp.float32)
    if cuts:
        entries = entries * block_levels(key, shape, cuts, -0.22, 0.18)
    return jnp.clip(entries, -reach, reach).astype(held_as)


def setup_inputs(seed: int = 0) -> dict:
    key_of = jax.random.split(jax.random.key(seed), 8)
    flow = draw_flow(jax.random.fold_in(key_of[7], 71), 0)
    adjoint = bell_draw(key_of[1], (5, LAYERS, NX, NT), 1.0, 6.0, ((2, 16), (3, 16)), jnp.float32)
    adjoint_later = bell_draw(key_of[2], (2, 5, LAYERS, NX, NT), 1.0, 6.0, ((3, 16), (4, 16)), jnp.float32)
    objective_grad = bell_draw(key_of[3], (5, LAYERS, NX, NT), 2.0, 12.0, ((2, 16), (3, 16)), jnp.float32)
    volume = jnp.clip(jnp.exp(math.log(2.0) - 1.3862944 * jax.random.uniform(key_of[4], (LAYERS, NX, NT), jnp.float32) ** block_levels(key_of[4], (LAYERS, NX, NT), ((1, 16), (2, 16)), -0.2, 0.2)), 0.5, 2.0)
    panel_maps = draw_panel_maps(jax.random.fold_in(key_of[7], 71), 0)
    rotor_step = jax.random.randint(key_of[6], (1,), 0, SECTORS * PHASES).astype(jnp.int32)
    return dict(flow=flow, adjoint=adjoint, adjoint_later=adjoint_later, objective_grad=objective_grad, volume=volume, panel_maps=panel_maps, rotor_step=rotor_step)


gamma_gas = 1.4
second_coef = 0.5
fourth_coef = 1.0 / 32.0
courant = 0.6
physical_step = 2.0
sensor_floor = 0.0001
highest = lax.Precision.HIGHEST

def pressure(state):
    density = state[0]
    kinetic = 0.5 * (state[1] * state[1] + state[2] * state[2] + state[3] * state[3]) / density
    return (gamma_gas - 1.0) * (state[4] - kinetic)

def slab(array, start, stop, axis):
    return lax.slice_in_dim(array, start, stop, axis=axis)

def direction_terms(wide, axis, momentum_row):
    density = wide[0]
    pressure_now = pressure(wide)
    speed = wide[momentum_row] / density
    sound_speed = jnp.sqrt(gamma_gas * pressure_now / density)
    radius = jnp.sqrt(speed * speed + 0.01) + sound_speed
    fluxes = [wide[momentum_row], wide[1] * speed, wide[2] * speed, wide[3] * speed, (wide[4] + pressure_now) * speed]
    fluxes[momentum_row] = fluxes[momentum_row] + pressure_now
    flux = jnp.stack(fluxes)
    scalar_axis = axis - 1
    length = pressure_now.shape[scalar_axis]
    upper_p = slab(pressure_now, 2, length, scalar_axis)
    middle_p = slab(pressure_now, 1, length - 1, scalar_axis)
    lower_p = slab(pressure_now, 0, length - 2, scalar_axis)
    bend = upper_p - 2.0 * middle_p + lower_p
    total = upper_p + 2.0 * middle_p + lower_p
    sensor = jnp.sqrt(bend * bend + sensor_floor) / total
    second_damp = second_coef * 0.5 * (slab(sensor, 0, length - 3, scalar_axis) + slab(sensor, 1, length - 2, scalar_axis))
    fourth_damp = fourth_coef * fourth_coef / (fourth_coef + second_damp)
    spectral = 0.5 * (slab(radius, 1, length - 2, scalar_axis) + slab(radius, 2, length - 1, scalar_axis))
    behind = slab(wide, 0, length - 3, axis)
    left_cell = slab(wide, 1, length - 2, axis)
    right_cell = slab(wide, 2, length - 1, axis)
    ahead = slab(wide, 3, length, axis)
    damping = spectral * (second_damp * (right_cell - left_cell) - fourth_damp * (ahead - 3.0 * right_cell + 3.0 * left_cell - behind))
    face = 0.5 * (slab(flux, 1, length - 2, axis) + slab(flux, 2, length - 1, axis)) - damping
    faces = length - 3
    change = slab(face, 1, faces, axis) - slab(face, 0, faces - 1, axis)
    return (change, slab(radius, 2, length - 2, scalar_axis))

def residual_and_radius(padded):
    full = jnp.pad(padded, ((0, 0), (2, 2), (0, 0), (0, 0)), mode='edge')
    axial_change, axial_radius = direction_terms(full[:, 2:-2, :, 2:-2], 2, 1)
    turning_change, turning_radius = direction_terms(full[:, 2:-2, 2:-2, :], 3, 2)
    radial_change, radial_radius = direction_terms(full[:, :, 2:-2, 2:-2], 1, 3)
    return (axial_change + turning_change + radial_change, axial_radius + turning_radius + radial_radius)

def apply_pair(nearer, farther, first_map, second_map):
    return jnp.einsum('...i,ti->...t', nearer, first_map, precision=highest) + jnp.einsum('...i,ti->...t', farther, second_map, precision=highest)

def interpolate(panel, first_map, second_map, near_shift, far_shift):
    sectors = panel.reshape(panel.shape[:-1] + (SECTORS, CIRC_DEV))
    order = jnp.arange(SECTORS, dtype=jnp.int32)
    nearer = jnp.take(sectors, ((order - near_shift) % SECTORS).astype(jnp.int32), axis=-2)
    farther = jnp.take(sectors, ((order - far_shift) % SECTORS).astype(jnp.int32), axis=-2)
    return apply_pair(nearer, farther, first_map, second_map).reshape(panel.shape)

def wrap_sides(column):
    return jnp.concatenate([column[..., -2:], column, column[..., :2]], axis=-1)

def reference(flow, adjoint, adjoint_later, objective_grad, volume, panel_maps, rotor_step):
    turn = rotor_step[0]
    offset = turn // PHASES
    maps = lax.dynamic_index_in_dim(panel_maps, turn % PHASES, 0, keepdims=False)
    half = NX // 2

    def whole_residual(state):
        rotor = state[:, :, :half]
        stator = state[:, :, half:]
        stator_ghost = interpolate(rotor[:, :, -2:], maps[0], maps[1], offset, offset + 1)
        rotor_ghost = interpolate(stator[:, :, :2], maps[2], maps[3], -offset, -offset - 1)
        inlet = jnp.repeat(rotor[:, :, :1], 2, axis=2)
        outlet = jnp.repeat(stator[:, :, -1:], 2, axis=2)
        rotor_change, rotor_radius = residual_and_radius(wrap_sides(jnp.concatenate([inlet, rotor, rotor_ghost], axis=2)))
        stator_change, stator_radius = residual_and_radius(wrap_sides(jnp.concatenate([stator_ghost, stator, outlet], axis=2)))
        return (jnp.concatenate([rotor_change, stator_change], axis=2), jnp.concatenate([rotor_radius, stator_radius], axis=1))
    change, pullback, radius_sum = jax.vjp(whole_residual, flow, has_aux=True)
    factor = courant / (radius_sum + 1.5 * courant * volume / physical_step)
    source = objective_grad + volume * (2.0 * adjoint_later[0] - 0.5 * adjoint_later[1]) / physical_step
    current = adjoint
    for sweep in range(ITERS):
        transposed, = pullback(current)
        current = current - factor * (1.5 * volume * current / physical_step + transposed - source)
    return current
```

```python
import functools

import jax
import jax.numpy as jnp
from jax import lax
from jax.experimental import pallas as pl
from jax.experimental.pallas import tpu as pltpu
from jax.sharding import PartitionSpec as P

PHASES = 4
ITERS = 4
ROUNDS = ITERS + 1
CHOICES = 16

FOURTH = 1.0 / 32.0
MESH = pl.DeviceIdType.MESH
HIGHEST = lax.Precision.HIGHEST

RINV, V1, V2, V3, ENTH, RP, RR, KE, NCELL = 0, 1, 2, 3, 4, 5, 6, 7, 8
LE2, LE4, DD, EE, N1, N0, RQ, NDIR = 0, 1, 2, 7, 12, 13, 14, 15


def cell_terms(u):
    rinv = 1.0 / u[0]
    v = [u[m] * rinv for m in (1, 2, 3)]
    ke = 0.5 * (v[0] * v[0] + v[1] * v[1] + v[2] * v[2])
    p = 0.4 * (u[4] - ke * u[0])
    c = jnp.sqrt(1.4 * p * rinv)
    return rinv, v, ke, p, c, 0.7 * rinv / c, -0.5 * c * rinv


def sensor_terms(below, here, above):
    bend = above - 2.0 * here + below
    tinv = 1.0 / (above + 2.0 * here + below)
    root = jnp.sqrt(bend * bend + 1e-4)
    nu = root * tinv
    by_bend = bend * tinv / root
    by_total = -nu * tinv
    return nu, 0.25 * (by_bend + by_total), 0.5 * (by_total - by_bend)


def face_terms(nu_low, nu_high, rad_low, rad_high, d1, d3):
    e2 = 0.25 * (nu_low + nu_high)
    e4 = FOURTH * FOURTH / (FOURTH + e2)
    lam = 0.5 * (rad_low + rad_high)
    slope = e4 * e4 * (1.0 / (FOURTH * FOURTH))
    dd = [-0.5 * (e2 * a - e4 * b) for a, b in zip(d1, d3)]
    ee = [-lam * (a + slope * b) for a, b in zip(d1, d3)]
    return [lam * e2, lam * e4] + dd + ee


def shifts(axis, length):
    def up(v):
        return pltpu.roll(v, length - 1, axis)

    def down(v):
        return pltpu.roll(v, 1, axis)

    return up, down


def direction_coefs(u, p, c, q, up, down):
    sq = jnp.sqrt(q * q + 0.01)
    radius = sq + c
    nu, n1, n0 = sensor_terms(down(p), p, up(p))
    d1 = [up(a) - a for a in u]
    d3 = [up(a) - 2.0 * a + down(a) for a in d1]
    faces = face_terms(nu, up(nu), radius, up(radius), d1, d3)
    return faces + [n1, n0, q / sq], radius


def dot5(a, b):
    return (a[0] * b[0] + a[1] * b[1]) + (a[2] * b[2] + a[3] * b[3]) + a[4] * b[4]


def direction_apply(lam, cf, cell, u, m, up, down):
    w = [a - up(a) for a in lam]
    lb = dot5(w, [cf(DD + v) for v in range(5)])
    eb = dot5(w, [cf(EE + v) for v in range(5)])
    rb = lb + down(lb)
    nub = eb + down(eb)
    t1 = nub * cf(N1)
    phi = [0.5 * (a + down(a)) for a in w]
    q = cell(V1 + m - 1)
    qb = rb * cf(RQ) + phi[1] * u(1) + phi[2] * u(2) + phi[3] * u(3) + phi[4] * cell(ENTH)
    pb = up(t1) + down(t1) + nub * cf(N0) + rb * cell(RP) + phi[4] * q + phi[m]
    le2, le4 = cf(LE2), cf(LE4)
    out = []
    for v in range(5):
        far = le4 * w[v]
        z = up(far) + down(far) - 2.0 * far - le2 * w[v]
        out.append(down(z) - z)
    qr = qb * cell(RINV)
    out[0] = out[0] + rb * cell(RR) - qr * q
    for v in range(1, 5):
        out[v] = out[v] + phi[v] * q
    out[m] = out[m] + phi[0] + qr
    return out, pb


def pressure_back(g, pb, cell):
    part = 0.4 * pb
    return [
        g[0] + part * cell(KE),
        g[1] - part * cell(V1),
        g[2] - part * cell(V2),
        g[3] - part * cell(V3),
        g[4] + part,
    ]


def kernel(
    base_offset,
    choices,
    step_ref,
    flow_ref,
    adjoint_ref,
    later_ref,
    objective_ref,
    volume_ref,
    maps_ref,
    out_ref,
    state,
    lam,
    cells,
    xcf,
    tcf,
    lcf,
    wcf,
    wcell,
    wu,
    grad,
    gradp,
    upd,
    edge_send,
    edge_recv,
    row_send,
    row_recv,
    flow_send,
    flow_recv,
    panel_send,
    panel_recv,
    ghost,
    send_sem,
    recv_sem,
    panel_send_sem,
    panel_recv_sem,
):
    sectors = lax.axis_size("sector")
    blocks = lax.axis_size("block")
    half = blocks // 2
    sec = lax.axis_index("sector")
    blk = lax.axis_index("block")
    right = lax.rem(sec + 1, sectors)
    left = lax.rem(sec + sectors - 1, sectors)
    slots = min(choices + 1, sectors)
    has_up = jnp.logical_and(blk != half - 1, blk != blocks - 1)
    has_down = jnp.logical_and(blk != 0, blk != half)
    on_rotor = blk == half - 1
    on_stator = blk == half
    on_face = jnp.logical_or(on_rotor, on_stator)
    turn = jnp.where(on_rotor, 1, -1)
    across = blk + turn

    def partner(slot):
        return lax.rem(sec + turn * (base_offset + slot) + 2 * sectors, sectors)

    barrier = pltpu.get_barrier_semaphore()

    def greet(sector, block):
        pl.semaphore_signal(
            barrier, inc=1, device_id={"sector": sector, "block": block}, device_id_type=MESH
        )

    greet(left, blk)
    greet(right, blk)

    @pl.when(has_up)
    def _():
        greet(sec, blk + 1)

    @pl.when(has_down)
    def _():
        greet(sec, blk - 1)

    @pl.when(on_face)
    def _():
        for slot in range(slots):
            greet(partner(slot), across)

    expected = (
        2
        + jnp.where(has_up, 1, 0)
        + jnp.where(has_down, 1, 0)
        + jnp.where(on_face, slots, 0)
    )

    def remote(src, dst, ssem, rsem, sector, block):
        return pltpu.make_async_remote_copy(
            src_ref=src,
            dst_ref=dst,
            send_sem=ssem,
            recv_sem=rsem,
            device_id={"sector": sector, "block": block},
            device_id_type=MESH,
        )

    def edge_copies(r):
        return (
            remote(edge_send.at[r], edge_recv.at[r, 1], send_sem.at[r, 0], recv_sem.at[r, 1], left, blk),
            remote(edge_send.at[r], edge_recv.at[r, 0], send_sem.at[r, 1], recv_sem.at[r, 0], right, blk),
        )

    def row_copies(r, src, dst):
        return (
            remote(src.at[0], dst.at[1], send_sem.at[r, 2], recv_sem.at[r, 3], sec, blk - 1),
            remote(src.at[1], dst.at[0], send_sem.at[r, 3], recv_sem.at[r, 2], sec, blk + 1),
        )

    def panel_copies(r):
        return [
            remote(
                panel_send.at[r],
                panel_recv.at[r, slot],
                panel_send_sem.at[r, slot],
                panel_recv_sem.at[r, slot],
                partner(slot),
                across,
            )
            for slot in range(slots)
        ]

    lane = lax.broadcasted_iota(jnp.int32, (8, 128), 1)
    place = lane & 15
    group = lane >> 4
    low_place = place < 8
    is_edge = jnp.logical_or(lane < 3, lane >= 125)

    def pack_edges(src, r):
        for v in range(5):
            packed = jnp.zeros((8, 128), jnp.float32)
            for g in range(8):
                tile = src[v, g // 2, (g % 2) * 8 : (g % 2) * 8 + 8, :]
                packed = jnp.where(group == g, pltpu.roll(tile, (16 * g + 8) % 128, 1), packed)
            edge_send[r, v] = packed

    def pack_rows(src, dst, width):
        for v in range(5):
            for l in range(4):
                rows = pl.ds(width * l, width)
                dst[0, v, rows, :] = src[v, l, 0:width, :]
                dst[1, v, rows, :] = src[v, l, 16 - width : 16, :]

    def unpack_edges(r, dst):
        for v in range(5):
            own = edge_send[r, v]
            dst[v, 4, 0:8, :] = jnp.where(low_place, own, edge_recv[r, 1, v])
            dst[v, 4, 8:16, :] = jnp.where(low_place, edge_recv[r, 0, v], own)

    for v in range(5):
        for l in range(4):
            state[v, l, 0:16, :] = flow_ref[v, l]
            lam[v, l, 0:16, :] = adjoint_ref[v, l]
            lam[v, l, 16:24, :] = jnp.zeros((8, 128), jnp.float32)
    pack_edges(state, 0)
    pack_rows(state, flow_send, 4)

    @pl.when(on_rotor)
    def _():
        for v in range(5):
            for l in range(4):
                panel_send[0, v, 2 * l : 2 * l + 2, :] = state[v, l, 14:16, :]

    @pl.when(on_stator)
    def _():
        for v in range(5):
            for l in range(4):
                panel_send[0, v, 2 * l : 2 * l + 2, :] = state[v, l, 0:2, :]

    pl.semaphore_wait(barrier, expected)

    @pl.when(on_face)
    def _():
        for copy in panel_copies(0):
            copy.start()

    for copy in edge_copies(0):
        copy.start()
    flow_down, flow_up = row_copies(0, flow_send, flow_recv)

    @pl.when(has_down)
    def _():
        flow_down.start()

    @pl.when(has_up)
    def _():
        flow_up.start()

    phase = lax.rem(step_ref[0], PHASES)
    choice = step_ref[0] // PHASES - base_offset

    def pick(r, wanted):
        out = panel_recv[r, 0]
        for slot in range(1, slots):
            out = jnp.where(wanted == slot, panel_recv[r, slot], out)
        return out.reshape(40, 128)

    def pick_pair(r):
        near = pick(r, choice)
        far = pick(r, choice + 1 if choices < sectors else lax.rem(choice + 1, sectors))
        return near, far

    for copy in edge_copies(0):
        copy.wait()
    unpack_edges(0, state)
    for v in range(5):
        state[v, 4, 16:24, :] = state[v, 4, 0:8, :]

    @pl.when(has_down)
    def _():
        flow_down.wait_send()
        remote(
            flow_send.at[1], flow_recv.at[0], send_sem.at[0, 3], recv_sem.at[0, 2], sec, blk - 1
        ).wait_recv()
        for v in range(5):
            for l in range(4):
                state[v, l, 20:24, :] = flow_recv[0, v, 4 * l : 4 * l + 4, :]

    @pl.when(has_up)
    def _():
        flow_up.wait_send()
        remote(
            flow_send.at[0], flow_recv.at[1], send_sem.at[0, 2], recv_sem.at[0, 3], sec, blk + 1
        ).wait_recv()
        for v in range(5):
            for l in range(4):
                state[v, l, 16:20, :] = flow_recv[1, v, 4 * l : 4 * l + 4, :]

    @pl.when(jnp.logical_not(has_down))
    def _():
        for v in range(5):
            for l in range(4):
                state[v, l, 20:24, :] = jnp.broadcast_to(state[v, l, 0:1, :], (4, 128))

    @pl.when(jnp.logical_not(has_up))
    def _():
        for v in range(5):
            for l in range(4):
                state[v, l, 16:20, :] = jnp.broadcast_to(state[v, l, 15:16, :], (4, 128))

    @pl.when(on_face)
    def _():
        for copy in panel_copies(0):
            copy.wait()
        near, far = pick_pair(0)
        first = jnp.where(on_rotor, 2, 0)
        dims = (((1,), (1,)), ((), ()))
        made = lax.dot_general(
            near, maps_ref[phase, first], dims, precision=HIGHEST, preferred_element_type=jnp.float32
        ) + lax.dot_general(
            far, maps_ref[phase, first + 1], dims, precision=HIGHEST, preferred_element_type=jnp.float32
        )
        ghost[...] = made.reshape(5, 8, 128)

    @pl.when(on_rotor)
    def _():
        for v in range(5):
            for l in range(4):
                state[v, l, 16:18, :] = ghost[v, 2 * l : 2 * l + 2, :]

    @pl.when(on_stator)
    def _():
        for v in range(5):
            for l in range(4):
                state[v, l, 22:24, :] = ghost[v, 2 * l : 2 * l + 2, :]

    x_up, x_down = shifts(0, 24)
    t_up, t_down = shifts(1, 128)
    w_up, w_down = shifts(0, 8)

    def set_cells(l, _):
        u = [state[v, l] for v in range(5)]
        rinv, vel, ke, p, c, rp, rr = cell_terms(u)
        for k, a in enumerate([rinv, vel[0], vel[1], vel[2], u[4] + p, rp, rr, ke]):
            cells[l, k] = a
        ut = [a[0:16] for a in u]
        cf, t_radius = direction_coefs(ut, p[0:16], c[0:16], vel[1][0:16], t_up, t_down)
        for k, a in enumerate(cf):
            tcf[l, k] = a
        return 0

    lax.fori_loop(0, 5, set_cells, 0)

    def set_x(l, _):
        u = [state[v, l] for v in range(5)]
        p = cells[l, ENTH] - u[4]
        vx = cells[l, V1]
        c = -2.0 * cells[l, RR] * u[0]
        cf, _ = direction_coefs(u, p, c, vx, x_up, x_down)
        for k, a in enumerate(cf):
            xcf[l, k] = a
        vol = volume_ref[l]
        rad = 3.0 * c[0:16]
        for k in (V1, V2, V3):
            q = cells[l, k, 0:16]
            rad = rad + jnp.sqrt(q * q + 0.01)
        factor = 0.6 / (rad + 0.45 * vol)
        upd[l, 0] = factor
        upd[l, 1] = 0.75 * factor * vol
        for v in range(5):
            source = objective_ref[v, l] + vol * (
                2.0 * later_ref[0, v, l] - 0.5 * later_ref[1, v, l]
            ) * 0.5
            upd[l, 2 + v] = factor * source
        return 0

    lax.fori_loop(0, 4, set_x, 0)

    def at_rows(half_at):
        return pl.ds(pl.multiple_of(half_at * 8, 8), 8)

    def set_l(half_at, _):
        rows = at_rows(half_at)
        u = [[state[v, l, rows, :] for v in range(5)] for l in range(4)]
        p = [cells[l, ENTH, rows, :] - u[l][4] for l in range(4)]
        q = [cells[l, V3, rows, :] for l in range(4)]
        sq = [jnp.sqrt(a * a + 0.01) for a in q]
        rad = [sq[l] - 2.0 * cells[l, RR, rows, :] * u[l][0] for l in range(4)]

        def clamp(l):
            return min(max(l, 0), 3)

        sens = [sensor_terms(p[clamp(j - 1)], p[clamp(j)], p[clamp(j + 1)]) for j in range(-1, 5)]
        zero = jnp.zeros((8, 128), jnp.float32)
        d1 = {f: [zero] * 5 for f in (-2, -1, 3, 4)}
        for f in range(3):
            d1[f] = [u[f + 1][v] - u[f][v] for v in range(5)]
        for f in range(-1, 4):
            d3 = [d1[f + 1][v] - 2.0 * d1[f][v] + d1[f - 1][v] for v in range(5)]
            faces = face_terms(
                sens[f + 1][0], sens[f + 2][0], rad[clamp(f)], rad[clamp(f + 1)], d1[f], d3
            )
            for k, a in enumerate(faces):
                lcf[f + 1, k, rows, :] = a
        for j in range(6):
            lcf[j, N1, rows, :] = sens[j][1]
            lcf[j, N0, rows, :] = sens[j][2]
        for l in range(4):
            lcf[l, RQ, rows, :] = q[l] / sq[l]
        return 0

    lax.fori_loop(0, 2, set_l, 0)

    at_end = jnp.logical_not(jnp.logical_and(has_up, has_down))
    low_end = jnp.logical_not(has_down)
    high_end = jnp.logical_not(has_up)

    @pl.when(low_end)
    def _():
        def window(ref, l, k):
            return jnp.concatenate([ref[l, k, 20:24, :], ref[l, k, 0:4, :]], axis=0)

        for l in range(4):
            for k in range(NDIR):
                wcf[l, k] = window(xcf, l, k)
            for k in range(NCELL):
                wcell[l, k] = window(cells, l, k)
            for v in range(1, 4):
                wu[l, v] = window(state, v, l)

    @pl.when(high_end)
    def _():
        for l in range(4):
            for k in range(NDIR):
                wcf[l, k] = xcf[l, k, 12:20, :]
            for k in range(NCELL):
                wcell[l, k] = cells[l, k, 12:20, :]
            for v in range(1, 4):
                wu[l, v] = state[v, l, 12:20, :]


    def iterate(k, _):
        r = k + 1
        pack_edges(lam, r)
        pack_rows(lam, row_send.at[r], 2)
        for copy in edge_copies(r):
            copy.start()
        to_down, to_up = row_copies(r, row_send.at[r], row_recv.at[r])

        @pl.when(has_down)
        def _():
            to_down.start()

        @pl.when(has_up)
        def _():
            to_up.start()

        @pl.when(at_end)
        def _():
            def end_rows(l, _):
                low = [jnp.concatenate([jnp.zeros((4, 128), jnp.float32), lam[v, l, 0:4, :]], axis=0) for v in range(5)]
                high = [jnp.concatenate([lam[v, l, 12:16, :], jnp.zeros((4, 128), jnp.float32)], axis=0) for v in range(5)]
                lw = [jnp.where(low_end, a, b) for a, b in zip(low, high)]
                g, pb = direction_apply(
                    lw,
                    lambda n: wcf[l, n],
                    lambda n: wcell[l, n],
                    lambda v: wu[l, v],
                    1,
                    w_up,
                    w_down,
                )
                g = pressure_back(g, pb, lambda n: wcell[l, n])
                for v in range(5):
                    wu[l, 4 + v] = g[v]
                return 0

            lax.fori_loop(0, 4, end_rows, 0)

        @pl.when(low_end)
        def _():
            for v in range(5):
                for l in range(4):
                    panel_send[r, v, 2 * l : 2 * l + 2, :] = wu[l, 4 + v, 2:4, :]

        @pl.when(high_end)
        def _():
            for v in range(5):
                for l in range(4):
                    panel_send[r, v, 2 * l : 2 * l + 2, :] = wu[l, 4 + v, 4:6, :]

        @pl.when(on_face)
        def _():
            for copy in panel_copies(r):
                copy.start()

        def apply_t(l):
            return direction_apply(
                [lam[v, l, 0:16, :] for v in range(5)],
                lambda n: tcf[l, n],
                lambda n: cells[l, n, 0:16, :],
                lambda v: state[v, l, 0:16, :],
                2,
                t_up,
                t_down,
            )

        lane16 = lax.broadcasted_iota(jnp.int32, (16, 128), 1)
        edge16 = jnp.logical_or(lane16 < 3, lane16 >= 125)

        def along_t(l, _):
            g, pb = apply_t(l)
            for v in range(5):
                grad[v, l] = jnp.where(edge16, 0.0, g[v])
            gradp[l] = jnp.where(edge16, 0.0, pb)
            return 0

        lax.fori_loop(0, 4, along_t, 0)

        def along_l(half_at, _):
            rows = at_rows(half_at)
            la = [[lam[v, l, rows, :] for v in range(5)] for l in range(4)]
            w = [[-a for a in la[0]]]
            for f in range(3):
                w.append([la[f][v] - la[f + 1][v] for v in range(5)])
            w.append(la[3])
            lb = [dot5(w[f], [lcf[f, DD + v, rows, :] for v in range(5)]) for f in range(5)]
            eb = [dot5(w[f], [lcf[f, EE + v, rows, :] for v in range(5)]) for f in range(5)]
            nub = [eb[0]] + [eb[f] + eb[f + 1] for f in range(4)] + [eb[4]]
            t1 = [nub[j] * lcf[j, N1, rows, :] for j in range(6)]
            t0 = [nub[j] * lcf[j, N0, rows, :] for j in range(6)]
            far = [[lcf[f, LE4, rows, :] * w[f][v] for v in range(5)] for f in range(5)]
            z = []
            for f in range(1, 4):
                z.append(
                    [
                        far[f - 1][v] + far[f + 1][v] - 2.0 * far[f][v] - lcf[f, LE2, rows, :] * w[f][v]
                        for v in range(5)
                    ]
                )
            for l in range(4):
                rb = lb[l] + lb[l + 1]
                phi = [0.5 * (w[l][v] + w[l + 1][v]) for v in range(5)]
                pb = t1[l] + t1[l + 2] + t0[l + 1]
                if l == 0:
                    rb = rb + lb[0]
                    phi = [phi[v] + 0.5 * w[0][v] for v in range(5)]
                    pb = pb + t1[1] + t0[0] + t1[0]
                if l == 3:
                    rb = rb + lb[4]
                    phi = [phi[v] + 0.5 * w[4][v] for v in range(5)]
                    pb = pb + t1[4] + t0[5] + t1[5]
                q = cells[l, V3, rows, :]
                qb = (
                    rb * lcf[l, RQ, rows, :]
                    + phi[1] * state[1, l, rows, :]
                    + phi[2] * state[2, l, rows, :]
                    + phi[3] * state[3, l, rows, :]
                    + phi[4] * cells[l, ENTH, rows, :]
                )
                pb = pb + rb * cells[l, RP, rows, :] + phi[4] * q + phi[3]
                if l == 0:
                    g = [-a for a in z[0]]
                elif l == 3:
                    g = list(z[2])
                else:
                    g = [a - b for a, b in zip(z[l - 1], z[l])]
                qr = qb * cells[l, RINV, rows, :]
                g[0] = g[0] + rb * cells[l, RR, rows, :] - qr * q
                for v in range(1, 5):
                    g[v] = g[v] + phi[v] * q
                g[3] = g[3] + phi[0] + qr
                for v in range(5):
                    grad[v, l, rows, :] += g[v]
                gradp[l, rows, :] += pb
            return 0

        lax.fori_loop(0, 2, along_l, 0)

        for copy in edge_copies(r):
            copy.wait()
        unpack_edges(r, lam)
        g, pb = apply_t(4)
        for v in range(5):
            grad[v, 4, 0:8, :] = jnp.where(low_place, g[v][0:8], g[v][8:16])
        gradp[4, 0:8, :] = jnp.where(low_place, pb[0:8], pb[8:16])

        @pl.when(has_down)
        def _():
            to_down.wait_send()
            remote(
                row_send.at[r, 1], row_recv.at[r, 0], send_sem.at[r, 3], recv_sem.at[r, 2], sec, blk - 1
            ).wait_recv()
            for v in range(5):
                for l in range(4):
                    lam[v, l, 22:24, :] = row_recv[r, 0, v, 2 * l : 2 * l + 2, :]

        @pl.when(has_up)
        def _():
            to_up.wait_send()
            remote(
                row_send.at[r, 0], row_recv.at[r, 1], send_sem.at[r, 2], recv_sem.at[r, 3], sec, blk + 1
            ).wait_recv()
            for v in range(5):
                for l in range(4):
                    lam[v, l, 16:18, :] = row_recv[r, 1, v, 2 * l : 2 * l + 2, :]

        def along_x(l, _):
            la = [lam[v, l] for v in range(5)]
            g, pb = direction_apply(
                la,
                lambda n: xcf[l, n],
                lambda n: cells[l, n],
                lambda v: state[v, l],
                1,
                x_up,
                x_down,
            )

            def spread(tile):
                parts = []
                for half_at in range(2):
                    by = lax.rem(248 - 32 * l - 16 * half_at, 128)
                    parts.append(jnp.where(is_edge, pltpu.roll(tile, by, 1), 0.0))
                return jnp.concatenate(parts, axis=0)

            g = [g[v][0:16] + grad[v, l] + spread(grad[v, 4, 0:8, :]) for v in range(5)]
            pb = pb[0:16] + gradp[l] + spread(gradp[4, 0:8, :])
            g = pressure_back(g, pb, lambda n: cells[l, n, 0:16, :])
            for v in range(5):
                old = la[v][0:16]
                lam[v, l, 0:16, :] = old - (upd[l, 1] * old + upd[l, 0] * g[v] - upd[l, 2 + v])
            return 0

        lax.fori_loop(0, 4, along_x, 0)

        @pl.when(on_face)
        def _():
            for copy in panel_copies(r):
                copy.wait()
            near, far = pick_pair(r)
            first = jnp.where(on_rotor, 0, 2)
            made = jnp.dot(
                near, maps_ref[phase, first], precision=HIGHEST, preferred_element_type=jnp.float32
            ) + jnp.dot(
                far, maps_ref[phase, first + 1], precision=HIGHEST, preferred_element_type=jnp.float32
            )
            ghost[...] = made.reshape(5, 8, 128)

        @pl.when(jnp.logical_and(at_end, jnp.logical_not(on_face)))
        def _():
            parity = lax.broadcasted_iota(jnp.int32, (8, 128), 0) & 1
            even = parity == 0
            keep = parity == jnp.where(low_end, 0, 1)
            for v in range(5):
                a = panel_send[r, v]
                both = a + jnp.where(even, pltpu.roll(a, 7, 0), pltpu.roll(a, 1, 0))
                ghost[v] = jnp.where(keep, both, 0.0)

        @pl.when(low_end)
        def _():
            for v in range(5):
                for l in range(4):
                    lam[v, l, 0:2, :] -= upd[l, 0, 0:2, :] * ghost[v, 2 * l : 2 * l + 2, :]

        @pl.when(high_end)
        def _():
            for v in range(5):
                for l in range(4):
                    lam[v, l, 14:16, :] -= upd[l, 0, 14:16, :] * ghost[v, 2 * l : 2 * l + 2, :]

        return 0

    lax.fori_loop(0, ITERS, iterate, 0)
    for v in range(5):
        for l in range(4):
            out_ref[v, l] = lam[v, l, 0:16, :]


def run(base_offset, choices, index, sectors, *args):
    slots = min(choices + 1, sectors)
    f32 = jnp.float32
    vmem = pl.BlockSpec(memory_space=pltpu.VMEM)
    return pl.pallas_call(
        functools.partial(kernel, base_offset, choices),
        out_shape=jax.ShapeDtypeStruct(args[1].shape, f32),
        in_specs=[pl.BlockSpec(memory_space=pltpu.SMEM)] + [vmem] * 6,
        out_specs=vmem,
        scratch_shapes=[
            pltpu.VMEM((5, 5, 24, 128), f32),
            pltpu.VMEM((5, 5, 24, 128), f32),
            pltpu.VMEM((5, NCELL, 24, 128), f32),
            pltpu.VMEM((4, NDIR, 24, 128), f32),
            pltpu.VMEM((5, NDIR, 16, 128), f32),
            pltpu.VMEM((6, NDIR, 16, 128), f32),
            pltpu.VMEM((4, NDIR, 8, 128), f32),
            pltpu.VMEM((4, NCELL, 8, 128), f32),
            pltpu.VMEM((4, 9, 8, 128), f32),
            pltpu.VMEM((5, 5, 16, 128), f32),
            pltpu.VMEM((5, 16, 128), f32),
            pltpu.VMEM((4, 7, 16, 128), f32),
            pltpu.VMEM((ROUNDS, 5, 8, 128), f32),
            pltpu.VMEM((ROUNDS, 2, 5, 8, 128), f32),
            pltpu.VMEM((ROUNDS, 2, 5, 8, 128), f32),
            pltpu.VMEM((ROUNDS, 2, 5, 8, 128), f32),
            pltpu.VMEM((2, 5, 16, 128), f32),
            pltpu.VMEM((2, 5, 16, 128), f32),
            pltpu.VMEM((ROUNDS, 5, 8, 128), f32),
            pltpu.VMEM((ROUNDS, slots, 5, 8, 128), f32),
            pltpu.VMEM((5, 8, 128), f32),
            pltpu.SemaphoreType.DMA((ROUNDS, 4)),
            pltpu.SemaphoreType.DMA((ROUNDS, 4)),
            pltpu.SemaphoreType.DMA((ROUNDS, slots)),
            pltpu.SemaphoreType.DMA((ROUNDS, slots)),
        ],
        compiler_params=pltpu.CompilerParams(collective_id=index, has_side_effects=True),
        name="adjoint_sweeps",
    )(*args)


def shards(flow, adjoint, adjoint_later, objective_grad, volume, panel_maps, rotor_step):
    sectors = lax.axis_size("sector")
    args = (rotor_step, flow, adjoint, adjoint_later, objective_grad, volume, panel_maps)
    choices = min(CHOICES, sectors)
    count = sectors // choices
    branches = [
        functools.partial(run, i * choices, choices, i, sectors) for i in range(count)
    ]
    if count == 1:
        return branches[0](*args)
    offset = rotor_step[0] // PHASES
    return lax.switch(offset // choices, branches, *args)


def solution(mesh):
    placed = (
        P(None, None, "block", "sector"),
        P(None, None, "block", "sector"),
        P(None, None, None, "block", "sector"),
        P(None, None, "block", "sector"),
        P(None, "block", "sector"),
        P(),
        P(),
    )
    return jax.shard_map(
        shards,
        mesh=mesh,
        in_specs=placed,
        out_specs=P(None, None, "block", "sector"),
        check_vma=False,
    )
```

```python
import functools

import jax
import jax.numpy as jnp
from jax import lax
from jax.experimental import pallas as pl
from jax.experimental.pallas import tpu as pltpu
from jax.sharding import PartitionSpec as P

PHASES = 4
ITERS = 4
ROUNDS = ITERS + 1
CHOICES = 1

FOURTH = 1.0 / 32.0
MESH = pl.DeviceIdType.MESH
HIGHEST = lax.Precision.HIGHEST

RINV, V1, V2, V3, ENTH, RP, RR, KE, NCELL = 0, 1, 2, 3, 4, 5, 6, 7, 8
LE2, LE4, DD, EE, N1, N0, RQ, NDIR = 0, 1, 2, 7, 12, 13, 14, 15


def cell_terms(u):
    rinv = 1.0 / u[0]
    v = [u[m] * rinv for m in (1, 2, 3)]
    ke = 0.5 * (v[0] * v[0] + v[1] * v[1] + v[2] * v[2])
    p = 0.4 * (u[4] - ke * u[0])
    c = jnp.sqrt(1.4 * p * rinv)
    return rinv, v, ke, p, c, 0.7 * rinv / c, -0.5 * c * rinv


def sensor_terms(below, here, above):
    bend = above - 2.0 * here + below
    tinv = 1.0 / (above + 2.0 * here + below)
    root = jnp.sqrt(bend * bend + 1e-4)
    nu = root * tinv
    by_bend = bend * tinv / root
    by_total = -nu * tinv
    return nu, 0.25 * (by_bend + by_total), 0.5 * (by_total - by_bend)


def face_terms(nu_low, nu_high, rad_low, rad_high, d1, d3):
    e2 = 0.25 * (nu_low + nu_high)
    e4 = FOURTH * FOURTH / (FOURTH + e2)
    lam = 0.5 * (rad_low + rad_high)
    slope = e4 * e4 * (1.0 / (FOURTH * FOURTH))
    dd = [-0.5 * (e2 * a - e4 * b) for a, b in zip(d1, d3)]
    ee = [-lam * (a + slope * b) for a, b in zip(d1, d3)]
    return [lam * e2, lam * e4] + dd + ee


def shifts(axis, length):
    def up(v):
        return pltpu.roll(v, length - 1, axis)

    def down(v):
        return pltpu.roll(v, 1, axis)

    return up, down


def direction_coefs(u, p, c, q, up, down):
    sq = jnp.sqrt(q * q + 0.01)
    radius = sq + c
    nu, n1, n0 = sensor_terms(down(p), p, up(p))
    d1 = [up(a) - a for a in u]
    d3 = [up(a) - 2.0 * a + down(a) for a in d1]
    faces = face_terms(nu, up(nu), radius, up(radius), d1, d3)
    return faces + [n1, n0, q / sq], radius


def dot5(a, b):
    return (a[0] * b[0] + a[1] * b[1]) + (a[2] * b[2] + a[3] * b[3]) + a[4] * b[4]


def direction_apply(lam, cf, cell, u, m, up, down):
    w = [a - up(a) for a in lam]
    lb = dot5(w, [cf(DD + v) for v in range(5)])
    eb = dot5(w, [cf(EE + v) for v in range(5)])
    rb = lb + down(lb)
    nub = eb + down(eb)
    t1 = nub * cf(N1)
    phi = [0.5 * (a + down(a)) for a in w]
    q = cell(V1 + m - 1)
    qb = rb * cf(RQ) + phi[1] * u(1) + phi[2] * u(2) + phi[3] * u(3) + phi[4] * cell(ENTH)
    pb = up(t1) + down(t1) + nub * cf(N0) + rb * cell(RP) + phi[4] * q + phi[m]
    le2, le4 = cf(LE2), cf(LE4)
    out = []
    for v in range(5):
        far = le4 * w[v]
        z = up(far) + down(far) - 2.0 * far - le2 * w[v]
        out.append(down(z) - z)
    qr = qb * cell(RINV)
    out[0] = out[0] + rb * cell(RR) - qr * q
    for v in range(1, 5):
        out[v] = out[v] + phi[v] * q
    out[m] = out[m] + phi[0] + qr
    return out, pb


def pressure_back(g, pb, cell):
    part = 0.4 * pb
    return [
        g[0] + part * cell(KE),
        g[1] - part * cell(V1),
        g[2] - part * cell(V2),
        g[3] - part * cell(V3),
        g[4] + part,
    ]


def kernel(
    base_offset,
    choices,
    step_ref,
    flow_ref,
    adjoint_ref,
    later_ref,
    objective_ref,
    volume_ref,
    maps_ref,
    out_ref,
    state,
    lam,
    cells,
    xcf,
    tcf,
    lcf,
    wcf,
    wcell,
    wu,
    grad,
    gradp,
    upd,
    edge_send,
    edge_recv,
    row_send,
    row_recv,
    flow_send,
    flow_recv,
    panel_send,
    panel_recv,
    ghost,
    send_sem,
    recv_sem,
    panel_send_sem,
    panel_recv_sem,
):
    sectors = lax.axis_size("sector")
    blocks = lax.axis_size("block")
    half = blocks // 2
    sec = lax.axis_index("sector")
    blk = lax.axis_index("block")
    right = lax.rem(sec + 1, sectors)
    left = lax.rem(sec + sectors - 1, sectors)
    slots = min(choices + 1, sectors)
    has_up = jnp.logical_and(blk != half - 1, blk != blocks - 1)
    has_down = jnp.logical_and(blk != 0, blk != half)
    on_rotor = blk == half - 1
    on_stator = blk == half
    on_face = jnp.logical_or(on_rotor, on_stator)
    turn = jnp.where(on_rotor, 1, -1)
    across = blk + turn

    def partner(slot):
        return lax.rem(sec + turn * (base_offset + slot) + 2 * sectors, sectors)

    barrier = pltpu.get_barrier_semaphore()

    def greet(sector, block):
        pl.semaphore_signal(
            barrier, inc=1, device_id={"sector": sector, "block": block}, device_id_type=MESH
        )

    greet(left, blk)
    greet(right, blk)

    @pl.when(has_up)
    def _():
        greet(sec, blk + 1)

    @pl.when(has_down)
    def _():
        greet(sec, blk - 1)

    @pl.when(on_face)
    def _():
        for slot in range(slots):
            greet(partner(slot), across)

    expected = (
        2
        + jnp.where(has_up, 1, 0)
        + jnp.where(has_down, 1, 0)
        + jnp.where(on_face, slots, 0)
    )

    def remote(src, dst, ssem, rsem, sector, block):
        return pltpu.make_async_remote_copy(
            src_ref=src,
            dst_ref=dst,
            send_sem=ssem,
            recv_sem=rsem,
            device_id={"sector": sector, "block": block},
            device_id_type=MESH,
        )

    def edge_copies(r):
        return (
            remote(edge_send.at[r], edge_recv.at[r, 1], send_sem.at[r, 0], recv_sem.at[r, 1], left, blk),
            remote(edge_send.at[r], edge_recv.at[r, 0], send_sem.at[r, 1], recv_sem.at[r, 0], right, blk),
        )

    def row_copies(r, src, dst):
        return (
            remote(src.at[0], dst.at[1], send_sem.at[r, 2], recv_sem.at[r, 3], sec, blk - 1),
            remote(src.at[1], dst.at[0], send_sem.at[r, 3], recv_sem.at[r, 2], sec, blk + 1),
        )

    def panel_copies(r):
        return [
            remote(
                panel_send.at[r],
                panel_recv.at[r, slot],
                panel_send_sem.at[r, slot],
                panel_recv_sem.at[r, slot],
                partner(slot),
                across,
            )
            for slot in range(slots)
        ]

    lane = lax.broadcasted_iota(jnp.int32, (8, 128), 1)
    place = lane & 15
    group = lane >> 4
    low_place = place < 8
    is_edge = jnp.logical_or(lane < 3, lane >= 125)

    def pack_edges(src, r):
        for v in range(5):
            packed = jnp.zeros((8, 128), jnp.float32)
            for g in range(8):
                tile = src[v, g // 2, (g % 2) * 8 : (g % 2) * 8 + 8, :]
                packed = jnp.where(group == g, pltpu.roll(tile, (16 * g + 8) % 128, 1), packed)
            edge_send[r, v] = packed

    def pack_rows(src, dst, width):
        for v in range(5):
            for l in range(4):
                rows = pl.ds(width * l, width)
                dst[0, v, rows, :] = src[v, l, 0:width, :]
                dst[1, v, rows, :] = src[v, l, 16 - width : 16, :]

    def unpack_edges(r, dst):
        for v in range(5):
            own = edge_send[r, v]
            dst[v, 4, 0:8, :] = jnp.where(low_place, own, edge_recv[r, 1, v])
            dst[v, 4, 8:16, :] = jnp.where(low_place, edge_recv[r, 0, v], own)

    for v in range(5):
        for l in range(4):
            state[v, l, 0:16, :] = flow_ref[v, l]
            lam[v, l, 0:16, :] = adjoint_ref[v, l]
            lam[v, l, 16:24, :] = jnp.zeros((8, 128), jnp.float32)
    pack_edges(state, 0)
    pack_rows(state, flow_send, 4)

    @pl.when(on_rotor)
    def _():
        for v in range(5):
            for l in range(4):
                panel_send[0, v, 2 * l : 2 * l + 2, :] = state[v, l, 14:16, :]

    @pl.when(on_stator)
    def _():
        for v in range(5):
            for l in range(4):
                panel_send[0, v, 2 * l : 2 * l + 2, :] = state[v, l, 0:2, :]

    pl.semaphore_wait(barrier, expected)

    @pl.when(on_face)
    def _():
        for copy in panel_copies(0):
            copy.start()

    for copy in edge_copies(0):
        copy.start()
    flow_down, flow_up = row_copies(0, flow_send, flow_recv)

    @pl.when(has_down)
    def _():
        flow_down.start()

    @pl.when(has_up)
    def _():
        flow_up.start()

    phase = lax.rem(step_ref[0], PHASES)
    choice = step_ref[0] // PHASES - base_offset

    def pick(r, wanted):
        out = panel_recv[r, 0]
        for slot in range(1, slots):
            out = jnp.where(wanted == slot, panel_recv[r, slot], out)
        return out.reshape(40, 128)

    def pick_pair(r):
        near = pick(r, choice)
        far = pick(r, choice + 1 if choices < sectors else lax.rem(choice + 1, sectors))
        return near, far

    for copy in edge_copies(0):
        copy.wait()
    unpack_edges(0, state)
    for v in range(5):
        state[v, 4, 16:24, :] = state[v, 4, 0:8, :]

    @pl.when(has_down)
    def _():
        flow_down.wait_send()
        remote(
            flow_send.at[1], flow_recv.at[0], send_sem.at[0, 3], recv_sem.at[0, 2], sec, blk - 1
        ).wait_recv()
        for v in range(5):
            for l in range(4):
                state[v, l, 20:24, :] = flow_recv[0, v, 4 * l : 4 * l + 4, :]

    @pl.when(has_up)
    def _():
        flow_up.wait_send()
        remote(
            flow_send.at[0], flow_recv.at[1], send_sem.at[0, 2], recv_sem.at[0, 3], sec, blk + 1
        ).wait_recv()
        for v in range(5):
            for l in range(4):
                state[v, l, 16:20, :] = flow_recv[1, v, 4 * l : 4 * l + 4, :]

    @pl.when(jnp.logical_not(has_down))
    def _():
        for v in range(5):
            for l in range(4):
                state[v, l, 20:24, :] = jnp.broadcast_to(state[v, l, 0:1, :], (4, 128))

    @pl.when(jnp.logical_not(has_up))
    def _():
        for v in range(5):
            for l in range(4):
                state[v, l, 16:20, :] = jnp.broadcast_to(state[v, l, 15:16, :], (4, 128))

    @pl.when(on_face)
    def _():
        for copy in panel_copies(0):
            copy.wait()
        near, far = pick_pair(0)
        first = jnp.where(on_rotor, 2, 0)
        dims = (((1,), (1,)), ((), ()))
        made = lax.dot_general(
            near, maps_ref[phase, first], dims, precision=HIGHEST, preferred_element_type=jnp.float32
        ) + lax.dot_general(
            far, maps_ref[phase, first + 1], dims, precision=HIGHEST, preferred_element_type=jnp.float32
        )
        ghost[...] = made.reshape(5, 8, 128)

    @pl.when(on_rotor)
    def _():
        for v in range(5):
            for l in range(4):
                state[v, l, 16:18, :] = ghost[v, 2 * l : 2 * l + 2, :]

    @pl.when(on_stator)
    def _():
        for v in range(5):
            for l in range(4):
                state[v, l, 22:24, :] = ghost[v, 2 * l : 2 * l + 2, :]

    x_up, x_down = shifts(0, 24)
    t_up, t_down = shifts(1, 128)
    w_up, w_down = shifts(0, 8)

    def set_cells(l, _):
        u = [state[v, l] for v in range(5)]
        rinv, vel, ke, p, c, rp, rr = cell_terms(u)
        for k, a in enumerate([rinv, vel[0], vel[1], vel[2], u[4] + p, rp, rr, ke]):
            cells[l, k] = a
        ut = [a[0:16] for a in u]
        cf, t_radius = direction_coefs(ut, p[0:16], c[0:16], vel[1][0:16], t_up, t_down)
        for k, a in enumerate(cf):
            tcf[l, k] = a
        return 0

    lax.fori_loop(0, 5, set_cells, 0)

    def set_x(l, _):
        u = [state[v, l] for v in range(5)]
        p = cells[l, ENTH] - u[4]
        vx = cells[l, V1]
        c = -2.0 * cells[l, RR] * u[0]
        cf, _ = direction_coefs(u, p, c, vx, x_up, x_down)
        for k, a in enumerate(cf):
            xcf[l, k] = a
        vol = volume_ref[l]
        rad = 3.0 * c[0:16]
        for k in (V1, V2, V3):
            q = cells[l, k, 0:16]
            rad = rad + jnp.sqrt(q * q + 0.01)
        factor = 0.6 / (rad + 0.45 * vol)
        upd[l, 0] = factor
        upd[l, 1] = 0.75 * factor * vol
        for v in range(5):
            source = objective_ref[v, l] + vol * (
                2.0 * later_ref[0, v, l] - 0.5 * later_ref[1, v, l]
            ) * 0.5
            upd[l, 2 + v] = factor * source
        return 0

    lax.fori_loop(0, 4, set_x, 0)

    def at_rows(half_at):
        return pl.ds(pl.multiple_of(half_at * 8, 8), 8)

    def set_l(half_at, _):
        rows = at_rows(half_at)
        u = [[state[v, l, rows, :] for v in range(5)] for l in range(4)]
        p = [cells[l, ENTH, rows, :] - u[l][4] for l in range(4)]
        q = [cells[l, V3, rows, :] for l in range(4)]
        sq = [jnp.sqrt(a * a + 0.01) for a in q]
        rad = [sq[l] - 2.0 * cells[l, RR, rows, :] * u[l][0] for l in range(4)]

        def clamp(l):
            return min(max(l, 0), 3)

        sens = [sensor_terms(p[clamp(j - 1)], p[clamp(j)], p[clamp(j + 1)]) for j in range(-1, 5)]
        zero = jnp.zeros((8, 128), jnp.float32)
        d1 = {f: [zero] * 5 for f in (-2, -1, 3, 4)}
        for f in range(3):
            d1[f] = [u[f + 1][v] - u[f][v] for v in range(5)]
        for f in range(-1, 4):
            d3 = [d1[f + 1][v] - 2.0 * d1[f][v] + d1[f - 1][v] for v in range(5)]
            faces = face_terms(
                sens[f + 1][0], sens[f + 2][0], rad[clamp(f)], rad[clamp(f + 1)], d1[f], d3
            )
            for k, a in enumerate(faces):
                lcf[f + 1, k, rows, :] = a
        for j in range(6):
            lcf[j, N1, rows, :] = sens[j][1]
            lcf[j, N0, rows, :] = sens[j][2]
        for l in range(4):
            lcf[l, RQ, rows, :] = q[l] / sq[l]
        return 0

    lax.fori_loop(0, 2, set_l, 0)

    at_end = jnp.logical_not(jnp.logical_and(has_up, has_down))
    low_end = jnp.logical_not(has_down)
    high_end = jnp.logical_not(has_up)

    @pl.when(low_end)
    def _():
        def window(ref, l, k):
            return jnp.concatenate([ref[l, k, 20:24, :], ref[l, k, 0:4, :]], axis=0)

        for l in range(4):
            for k in range(NDIR):
                wcf[l, k] = window(xcf, l, k)
            for k in range(NCELL):
                wcell[l, k] = window(cells, l, k)
            for v in range(1, 4):
                wu[l, v] = window(state, v, l)

    @pl.when(high_end)
    def _():
        for l in range(4):
            for k in range(NDIR):
                wcf[l, k] = xcf[l, k, 12:20, :]
            for k in range(NCELL):
                wcell[l, k] = cells[l, k, 12:20, :]
            for v in range(1, 4):
                wu[l, v] = state[v, l, 12:20, :]


    def iterate(k, _):
        r = k + 1
        pack_edges(lam, r)
        pack_rows(lam, row_send.at[r], 2)
        for copy in edge_copies(r):
            copy.start()
        to_down, to_up = row_copies(r, row_send.at[r], row_recv.at[r])

        @pl.when(has_down)
        def _():
            to_down.start()

        @pl.when(has_up)
        def _():
            to_up.start()

        @pl.when(at_end)
        def _():
            def end_rows(l, _):
                low = [jnp.concatenate([jnp.zeros((4, 128), jnp.float32), lam[v, l, 0:4, :]], axis=0) for v in range(5)]
                high = [jnp.concatenate([lam[v, l, 12:16, :], jnp.zeros((4, 128), jnp.float32)], axis=0) for v in range(5)]
                lw = [jnp.where(low_end, a, b) for a, b in zip(low, high)]
                g, pb = direction_apply(
                    lw,
                    lambda n: wcf[l, n],
                    lambda n: wcell[l, n],
                    lambda v: wu[l, v],
                    1,
                    w_up,
                    w_down,
                )
                g = pressure_back(g, pb, lambda n: wcell[l, n])
                for v in range(5):
                    wu[l, 4 + v] = g[v]
                return 0

            lax.fori_loop(0, 4, end_rows, 0)

        @pl.when(low_end)
        def _():
            for v in range(5):
                for l in range(4):
                    panel_send[r, v, 2 * l : 2 * l + 2, :] = wu[l, 4 + v, 2:4, :]

        @pl.when(high_end)
        def _():
            for v in range(5):
                for l in range(4):
                    panel_send[r, v, 2 * l : 2 * l + 2, :] = wu[l, 4 + v, 4:6, :]

        @pl.when(on_face)
        def _():
            for copy in panel_copies(r):
                copy.start()

        def apply_t(l):
            return direction_apply(
                [lam[v, l, 0:16, :] for v in range(5)],
                lambda n: tcf[l, n],
                lambda n: cells[l, n, 0:16, :],
                lambda v: state[v, l, 0:16, :],
                2,
                t_up,
                t_down,
            )

        lane16 = lax.broadcasted_iota(jnp.int32, (16, 128), 1)
        edge16 = jnp.logical_or(lane16 < 3, lane16 >= 125)

        def along_t(l, _):
            g, pb = apply_t(l)
            for v in range(5):
                grad[v, l] = jnp.where(edge16, 0.0, g[v])
            gradp[l] = jnp.where(edge16, 0.0, pb)
            return 0

        lax.fori_loop(0, 4, along_t, 0)

        def along_l(half_at, _):
            rows = at_rows(half_at)
            la = [[lam[v, l, rows, :] for v in range(5)] for l in range(4)]
            w = [[-a for a in la[0]]]
            for f in range(3):
                w.append([la[f][v] - la[f + 1][v] for v in range(5)])
            w.append(la[3])
            lb = [dot5(w[f], [lcf[f, DD + v, rows, :] for v in range(5)]) for f in range(5)]
            eb = [dot5(w[f], [lcf[f, EE + v, rows, :] for v in range(5)]) for f in range(5)]
            nub = [eb[0]] + [eb[f] + eb[f + 1] for f in range(4)] + [eb[4]]
            t1 = [nub[j] * lcf[j, N1, rows, :] for j in range(6)]
            t0 = [nub[j] * lcf[j, N0, rows, :] for j in range(6)]
            far = [[lcf[f, LE4, rows, :] * w[f][v] for v in range(5)] for f in range(5)]
            z = []
            for f in range(1, 4):
                z.append(
                    [
                        far[f - 1][v] + far[f + 1][v] - 2.0 * far[f][v] - lcf[f, LE2, rows, :] * w[f][v]
                        for v in range(5)
                    ]
                )
            for l in range(4):
                rb = lb[l] + lb[l + 1]
                phi = [0.5 * (w[l][v] + w[l + 1][v]) for v in range(5)]
                pb = t1[l] + t1[l + 2] + t0[l + 1]
                if l == 0:
                    rb = rb + lb[0]
                    phi = [phi[v] + 0.5 * w[0][v] for v in range(5)]
                    pb = pb + t1[1] + t0[0] + t1[0]
                if l == 3:
                    rb = rb + lb[4]
                    phi = [phi[v] + 0.5 * w[4][v] for v in range(5)]
                    pb = pb + t1[4] + t0[5] + t1[5]
                q = cells[l, V3, rows, :]
                qb = (
                    rb * lcf[l, RQ, rows, :]
                    + phi[1] * state[1, l, rows, :]
                    + phi[2] * state[2, l, rows, :]
                    + phi[3] * state[3, l, rows, :]
                    + phi[4] * cells[l, ENTH, rows, :]
                )
                pb = pb + rb * cells[l, RP, rows, :] + phi[4] * q + phi[3]
                if l == 0:
                    g = [-a for a in z[0]]
                elif l == 3:
                    g = list(z[2])
                else:
                    g = [a - b for a, b in zip(z[l - 1], z[l])]
                qr = qb * cells[l, RINV, rows, :]
                g[0] = g[0] + rb * cells[l, RR, rows, :] - qr * q
                for v in range(1, 5):
                    g[v] = g[v] + phi[v] * q
                g[3] = g[3] + phi[0] + qr
                for v in range(5):
                    grad[v, l, rows, :] += g[v]
                gradp[l, rows, :] += pb
            return 0

        lax.fori_loop(0, 2, along_l, 0)

        for copy in edge_copies(r):
            copy.wait()
        unpack_edges(r, lam)
        g, pb = apply_t(4)
        for v in range(5):
            grad[v, 4, 0:8, :] = jnp.where(low_place, g[v][0:8], g[v][8:16])
        gradp[4, 0:8, :] = jnp.where(low_place, pb[0:8], pb[8:16])

        @pl.when(has_down)
        def _():
            to_down.wait_send()
            remote(
                row_send.at[r, 1], row_recv.at[r, 0], send_sem.at[r, 3], recv_sem.at[r, 2], sec, blk - 1
            ).wait_recv()
            for v in range(5):
                for l in range(4):
                    lam[v, l, 22:24, :] = row_recv[r, 0, v, 2 * l : 2 * l + 2, :]

        @pl.when(has_up)
        def _():
            to_up.wait_send()
            remote(
                row_send.at[r, 0], row_recv.at[r, 1], send_sem.at[r, 2], recv_sem.at[r, 3], sec, blk + 1
            ).wait_recv()
            for v in range(5):
                for l in range(4):
                    lam[v, l, 16:18, :] = row_recv[r, 1, v, 2 * l : 2 * l + 2, :]

        def along_x(l, _):
            la = [lam[v, l] for v in range(5)]
            g, pb = direction_apply(
                la,
                lambda n: xcf[l, n],
                lambda n: cells[l, n],
                lambda v: state[v, l],
                1,
                x_up,
                x_down,
            )

            def spread(tile):
                parts = []
                for half_at in range(2):
                    by = lax.rem(248 - 32 * l - 16 * half_at, 128)
                    parts.append(jnp.where(is_edge, pltpu.roll(tile, by, 1), 0.0))
                return jnp.concatenate(parts, axis=0)

            g = [g[v][0:16] + grad[v, l] + spread(grad[v, 4, 0:8, :]) for v in range(5)]
            pb = pb[0:16] + gradp[l] + spread(gradp[4, 0:8, :])
            g = pressure_back(g, pb, lambda n: cells[l, n, 0:16, :])
            for v in range(5):
                old = la[v][0:16]
                lam[v, l, 0:16, :] = old - (upd[l, 1] * old + upd[l, 0] * g[v] - upd[l, 2 + v])
            return 0

        lax.fori_loop(0, 4, along_x, 0)

        @pl.when(on_face)
        def _():
            for copy in panel_copies(r):
                copy.wait()
            near, far = pick_pair(r)
            first = jnp.where(on_rotor, 0, 2)
            made = jnp.dot(
                near, maps_ref[phase, first], precision=HIGHEST, preferred_element_type=jnp.float32
            ) + jnp.dot(
                far, maps_ref[phase, first + 1], precision=HIGHEST, preferred_element_type=jnp.float32
            )
            ghost[...] = made.reshape(5, 8, 128)

        @pl.when(jnp.logical_and(at_end, jnp.logical_not(on_face)))
        def _():
            parity = lax.broadcasted_iota(jnp.int32, (8, 128), 0) & 1
            even = parity == 0
            keep = parity == jnp.where(low_end, 0, 1)
            for v in range(5):
                a = panel_send[r, v]
                both = a + jnp.where(even, pltpu.roll(a, 7, 0), pltpu.roll(a, 1, 0))
                ghost[v] = jnp.where(keep, both, 0.0)

        @pl.when(low_end)
        def _():
            for v in range(5):
                for l in range(4):
                    lam[v, l, 0:2, :] -= upd[l, 0, 0:2, :] * ghost[v, 2 * l : 2 * l + 2, :]

        @pl.when(high_end)
        def _():
            for v in range(5):
                for l in range(4):
                    lam[v, l, 14:16, :] -= upd[l, 0, 14:16, :] * ghost[v, 2 * l : 2 * l + 2, :]

        return 0

    lax.fori_loop(0, ITERS, iterate, 0)
    for v in range(5):
        for l in range(4):
            out_ref[v, l] = lam[v, l, 0:16, :]


def run(base_offset, choices, index, sectors, *args):
    slots = min(choices + 1, sectors)
    f32 = jnp.float32
    vmem = pl.BlockSpec(memory_space=pltpu.VMEM)
    return pl.pallas_call(
        functools.partial(kernel, base_offset, choices),
        out_shape=jax.ShapeDtypeStruct(args[1].shape, f32),
        in_specs=[pl.BlockSpec(memory_space=pltpu.SMEM)] + [vmem] * 6,
        out_specs=vmem,
        scratch_shapes=[
            pltpu.VMEM((5, 5, 24, 128), f32),
            pltpu.VMEM((5, 5, 24, 128), f32),
            pltpu.VMEM((5, NCELL, 24, 128), f32),
            pltpu.VMEM((4, NDIR, 24, 128), f32),
            pltpu.VMEM((5, NDIR, 16, 128), f32),
            pltpu.VMEM((6, NDIR, 16, 128), f32),
            pltpu.VMEM((4, NDIR, 8, 128), f32),
            pltpu.VMEM((4, NCELL, 8, 128), f32),
            pltpu.VMEM((4, 9, 8, 128), f32),
            pltpu.VMEM((5, 5, 16, 128), f32),
            pltpu.VMEM((5, 16, 128), f32),
            pltpu.VMEM((4, 7, 16, 128), f32),
            pltpu.VMEM((ROUNDS, 5, 8, 128), f32),
            pltpu.VMEM((ROUNDS, 2, 5, 8, 128), f32),
            pltpu.VMEM((ROUNDS, 2, 5, 8, 128), f32),
            pltpu.VMEM((ROUNDS, 2, 5, 8, 128), f32),
            pltpu.VMEM((2, 5, 16, 128), f32),
            pltpu.VMEM((2, 5, 16, 128), f32),
            pltpu.VMEM((ROUNDS, 5, 8, 128), f32),
            pltpu.VMEM((ROUNDS, slots, 5, 8, 128), f32),
            pltpu.VMEM((5, 8, 128), f32),
            pltpu.SemaphoreType.DMA((ROUNDS, 4)),
            pltpu.SemaphoreType.DMA((ROUNDS, 4)),
            pltpu.SemaphoreType.DMA((ROUNDS, slots)),
            pltpu.SemaphoreType.DMA((ROUNDS, slots)),
        ],
        compiler_params=pltpu.CompilerParams(collective_id=index, has_side_effects=True),
        name="adjoint_sweeps",
    )(*args)


def shards(flow, adjoint, adjoint_later, objective_grad, volume, panel_maps, rotor_step):
    sectors = lax.axis_size("sector")
    args = (rotor_step, flow, adjoint, adjoint_later, objective_grad, volume, panel_maps)
    choices = min(CHOICES, sectors)
    count = sectors // choices
    branches = [
        functools.partial(run, i * choices, choices, i, sectors) for i in range(count)
    ]
    if count == 1:
        return branches[0](*args)
    offset = rotor_step[0] // PHASES
    return lax.switch(offset // choices, branches, *args)


def solution(mesh):
    placed = (
        P(None, None, "block", "sector"),
        P(None, None, "block", "sector"),
        P(None, None, None, "block", "sector"),
        P(None, None, "block", "sector"),
        P(None, "block", "sector"),
        P(),
        P(),
    )
    return jax.shard_map(
        shards,
        mesh=mesh,
        in_specs=placed,
        out_specs=P(None, None, "block", "sector"),
        check_vma=False,
    )
```
